32 devices in a mesh: src: 2 (over x), tgt: 16 (over z, y, core).
Axes of the slice: x: 2, y: 2, z: 4, core: 2. Of those that a mesh axis runs over, the one named last changes fastest.
Arguments:
- src_emb: bfloat16 [8192, 256], P(('src', 'tgt')), may hold values from -32 to 32
- tgt_emb: bfloat16 [16384, 256], P(('tgt', 'src')), may hold values from -32 to 32
- block_rows: int32 [2, 16, 24], P('src', 'tgt'), may hold values from 0 to 15, as said below
- block_cols: int32 [2, 16, 24], P('src', 'tgt'), may hold values from 0 to 3
- block_counts: int32 [2, 16], P('src', 'tgt'), may hold values from 4 to 24, as said below
Outputs:
- transport: bfloat16 [2, 16, 24, 256, 256], P('src', 'tgt')
- row_potential: float32 [8192], P(('src', 'tgt'))
- col_potential: float32 [16384], P(('tgt', 'src'))
The draws below stay inside these ranges and needn't reach their ends.
Inputs may be any that keep to these rules, and one draw needn't show every extreme that they name: The 24 slots of one device name distinct blocks (block_rows, block_cols); its first 4 slots name every local block column once; every local block row of a src index is named by a live slot of some device of that index. `block_counts`: exactly 24 on some device.
All inputs are finite; a program needn't handle non-finite values.
Results may differ from the reference program's by a relative error of at most 0.0019.
The reference program's roundings to bfloat16 on the way (of `src_unit` and `tgt_unit`) count: a program that leaves them out, or rounds other values in their place, can miss the bound.
Values may be sent and summed in bfloat16 or wider, within the bound.
No kernel may reach another device: no remote copies, remote signals or barrier semaphores. Data moves between devices by JAX's collectives and lax.ppermute only.
A program may use at most 64 MiB of HBM per device.

```python
import math
import jax
import jax.numpy as jnp
from jax import lax

DIM = 256
BLOCK = 256
ROW_BLOCKS = 16
COL_BLOCKS = 4
SLOTS = 24
ITERS = 3
SOURCES = 8192
TARGETS = 16384
N_SRC = 2
N_TGT = 16


def pattern_parts(key):
    base_key = jax.random.fold_in(key, 7)
    devices = N_SRC * N_TGT
    offsets = jax.random.randint(jax.random.fold_in(base_key, 1), (N_SRC,), 0, ROW_BLOCKS)
    positions = jnp.arange(ROW_BLOCKS * COL_BLOCKS, dtype=jnp.int32)
    pos_row = positions // COL_BLOCKS
    pos_col = positions % COL_BLOCKS

    def per_device(device):
        source = device // N_TGT
        target = device % N_TGT
        rank_order = jax.random.permutation(jax.random.fold_in(base_key, 100 + device), ROW_BLOCKS * COL_BLOCKS).astype(jnp.int32)
        diagonal = pos_row == (target * COL_BLOCKS + pos_col + offsets[source]) % ROW_BLOCKS
        sort_keys = jnp.where(diagonal, pos_col, COL_BLOCKS + rank_order)
        ordering = jnp.argsort(sort_keys)[:SLOTS].astype(jnp.int32)
        return (ordering // COL_BLOCKS, ordering % COL_BLOCKS)
    slot_rows, slot_cols = jax.vmap(per_device)(jnp.arange(devices, dtype=jnp.int32))
    uniform_ints = jax.random.randint(jax.random.fold_in(base_key, 2), (devices,), 0, 1001)
    extra_slots = (SLOTS - COL_BLOCKS) * (uniform_ints * uniform_ints // 1000) * uniform_ints // 1000000
    busiest = jax.random.randint(jax.random.fold_in(base_key, 3), (), 0, devices)
    counts = COL_BLOCKS + jnp.where(jnp.arange(devices, dtype=jnp.int32) == busiest, SLOTS - COL_BLOCKS, extra_slots)
    return (slot_rows.reshape(N_SRC, N_TGT, SLOTS).astype(jnp.int32), slot_cols.reshape(N_SRC, N_TGT, SLOTS).astype(jnp.int32), counts.reshape(N_SRC, N_TGT).astype(jnp.int32))


def target_base(key):
    entries = jax.random.normal(jax.random.fold_in(key, 21), (TARGETS, DIM), jnp.float32)
    scales = jnp.exp(jax.random.uniform(jax.random.fold_in(key, 22), (TARGETS, 1), jnp.float32, math.log(0.5), math.log(4.0)))
    return (entries, scales)


def draw_tgt_emb(key, part):
    entries, scales = target_base(key)
    table = entries * scales
    return jnp.clip(table, -32.0, 32.0).astype(jnp.bfloat16)


def draw_src_emb(key, part):
    entries = jax.random.normal(jax.random.fold_in(key, 31), (SOURCES, DIM), jnp.float32)
    scales = jnp.exp(jax.random.uniform(jax.random.fold_in(key, 32), (SOURCES, 1), jnp.float32, math.log(0.5), math.log(4.0)))
    table = entries * scales
    return jnp.clip(table, -32.0, 32.0).astype(jnp.bfloat16)


def draw_block_rows(key, part):
    return pattern_parts(key)[0]


def draw_block_cols(key, part):
    return pattern_parts(key)[1]


def draw_block_counts(key, part):
    return pattern_parts(key)[2]


def setup_inputs(seed: int = 0) -> dict:
    keys = jax.random.split(jax.random.key(seed), 6)
    return {
        "src_emb": draw_src_emb(jax.random.fold_in(keys[5], 71), 0),
        "tgt_emb": draw_tgt_emb(jax.random.fold_in(keys[5], 71), 0),
        "block_rows": draw_block_rows(jax.random.fold_in(keys[5], 71), 0),
        "block_cols": draw_block_cols(jax.random.fold_in(keys[5], 71), 0),
        "block_counts": draw_block_counts(jax.random.fold_in(keys[5], 71), 0),
    }


inv_temp = 250.0
sentinel = -1e+30
highest = lax.Precision.HIGHEST

def unit_rows(embedding):
    values = embedding.astype(jnp.float32)
    inverse_norm = lax.rsqrt(lax.optimization_barrier(jnp.sum(values * values, axis=1, keepdims=True)) + 1e-06)
    return (values * inverse_norm).astype(jnp.bfloat16)

def reference(src_emb, tgt_emb, block_rows, block_cols, block_counts):
    src_unit = unit_rows(src_emb).reshape(N_SRC, ROW_BLOCKS, BLOCK, DIM)
    tgt_unit = unit_rows(tgt_emb).reshape(N_TGT, COL_BLOCKS, BLOCK, DIM)
    slot_ids = jnp.arange(SLOTS, dtype=jnp.int32)
    live_slot = slot_ids[None, None, :] < block_counts[:, :, None]
    row_hot = ((block_rows[..., None] == jnp.arange(ROW_BLOCKS, dtype=jnp.int32)) & live_slot[..., None]).astype(jnp.float32)
    col_hot = ((block_cols[..., None] == jnp.arange(COL_BLOCKS, dtype=jnp.int32)) & live_slot[..., None]).astype(jnp.float32)
    tgt_index = jnp.arange(N_TGT, dtype=jnp.int32)[:, None]
    sources = jnp.arange(N_SRC, dtype=jnp.int32)
    log_ratio = math.log(SOURCES / TARGETS)

    def tile_scores(source):
        src_blocks = src_unit[source][block_rows[source]].astype(jnp.float32)
        tgt_blocks = tgt_unit[tgt_index, block_cols[source]].astype(jnp.float32)
        products = jnp.einsum('tcbe,tcde->tcbd', src_blocks, tgt_blocks, precision=highest)
        return jnp.where(live_slot[source][:, :, None, None], products * inv_temp, sentinel)
    scores = lax.map(tile_scores, sources)

    def row_pass(col_dual):

        def per_source(source):
            col_slots = col_dual[tgt_index, block_cols[source]]
            shifted = scores[source] + col_slots[:, :, None, :]
            slot_max = lax.optimization_barrier(jnp.max(shifted, axis=3))
            slot_hot = row_hot[source]
            top_value = lax.optimization_barrier(jnp.max(jnp.where(slot_hot[..., None] > 0, slot_max[:, :, None, :], sentinel), axis=(0, 1)))
            top_slots = top_value[block_rows[source]]
            slot_sums = lax.optimization_barrier(jnp.sum(jnp.exp(shifted - top_slots[..., None]), axis=3))
            sum_total = jnp.einsum('tcr,tcb->rb', slot_hot, slot_sums, precision=highest)
            return -(top_value + jnp.log(sum_total))
        return lax.map(per_source, sources)

    def col_pass(row_dual):

        def shifted_of(source):
            row_slots = row_dual[source][block_rows[source]]
            return scores[source] + row_slots[:, :, :, None]

        def local_top(source):
            slot_max = lax.optimization_barrier(jnp.max(shifted_of(source), axis=2))
            slot_hot = col_hot[source]
            return lax.optimization_barrier(jnp.max(jnp.where(slot_hot[..., None] > 0, slot_max[:, :, None, :], sentinel), axis=1))
        top_value = lax.optimization_barrier(jnp.max(lax.map(local_top, sources), axis=0))

        def local_sum(source):
            top_slots = top_value[tgt_index, block_cols[source]]
            slot_sums = lax.optimization_barrier(jnp.sum(jnp.exp(shifted_of(source) - top_slots[:, :, None, :]), axis=2))
            return jnp.einsum('tcn,tcb->tnb', col_hot[source], slot_sums, precision=highest)
        sum_total = lax.optimization_barrier(jnp.sum(lax.map(local_sum, sources), axis=0))
        return log_ratio - (top_value + jnp.log(sum_total))
    col_dual = jnp.zeros((N_TGT, COL_BLOCKS, BLOCK), jnp.float32)
    row_dual = jnp.zeros((N_SRC, ROW_BLOCKS, BLOCK), jnp.float32)
    for sweep in range(ITERS):
        row_dual = row_pass(col_dual)
        col_dual = col_pass(row_dual)

    def plan_of(source):
        row_slots = row_dual[source][block_rows[source]]
        col_slots = col_dual[tgt_index, block_cols[source]]
        return jnp.exp(scores[source] + row_slots[..., None] + col_slots[:, :, None, :]).astype(jnp.bfloat16)
    transport = lax.map(plan_of, sources)
    return (transport, (row_dual / inv_temp).reshape(SOURCES), (col_dual / inv_temp).reshape(TARGETS))
```

```python
import functools
import math

import jax
import jax.numpy as jnp
from jax import lax
from jax.experimental import pallas as pl
from jax.experimental.pallas import tpu as pltpu
from jax.sharding import PartitionSpec as P

BLOCK = 256
ROW_BLOCKS = 16
COL_BLOCKS = 4
ITERS = 3
LANES = 128
SUB = 8

inv_temp = 250.0
sentinel = -1e30
log2e = math.log2(math.e)
ln2 = math.log(2.0)

VM = pl.BlockSpec(memory_space=pltpu.VMEM)
SM = pl.BlockSpec(memory_space=pltpu.SMEM)
ANY = pl.BlockSpec(memory_space=pl.ANY)


def unit_rows(embedding):
    values = embedding.astype(jnp.float32)
    inverse_norm = lax.rsqrt(jnp.sum(values * values, axis=1, keepdims=True) + 1e-06)
    return (values * inverse_norm).astype(jnp.bfloat16)


def swap(value, axis, key):
    size = lax.axis_size(axis)
    return lax.ppermute(value, axis, [(i, i ^ key) for i in range(size)])


def rounds_of(size):
    groups = []
    bit = 1
    while bit < size:
        if bit * 2 < size:
            groups.append((bit, 2 * bit, 3 * bit))
            bit *= 4
        else:
            groups.append((bit,))
            bit *= 2
    return groups


def merge_lse(parts):
    top = functools.reduce(jnp.maximum, parts)
    total = functools.reduce(jnp.add, [jnp.exp2(part - top) for part in parts])
    return top + jnp.log2(total)


def total_lse(local, axis):
    for keys in rounds_of(lax.axis_size(axis)):
        local = merge_lse([local] + [swap(local, axis, key) for key in keys])
    return local


def gather_rows(rows, axis):
    size = lax.axis_size(axis)
    groups = []
    bit = size
    held = [((0,), rows)]
    first = True
    while bit > 1:
        if first and bit >= 4:
            keys = (bit // 4, bit // 2, 3 * (bit // 4))
            bit //= 4
        else:
            keys = (bit // 2,)
            bit //= 2
        if first:
            news = [((key,), swap(rows, axis, key)) for key in keys]
            if len(news) > 1:
                news = [(sum((o for o, _ in news), ()), jnp.concatenate([r for _, r in news], 0))]
            first = False
        else:
            news = []
            for offsets, stack in held:
                for key in keys:
                    news.append((tuple(o ^ key for o in offsets), swap(stack, axis, key)))
        held = held + news
    return held


def first_pass_kernel(layout, share_src, share_tgt, meta, *refs):
    n_src, n_tgt = len(layout[0]), len(layout[1])
    src_parts = refs[:n_src]
    tgt_parts = refs[n_src : n_src + n_tgt]
    scores, lse, src_all, tgt_all, top, tot, sem = refs[n_src + n_tgt :]
    rows_at, cols_at, count, src_pos, tgt_pos = meta
    copies = []
    for parts, offsets_list, dest, pos, share in (
        (src_parts, layout[0], src_all, src_pos[0], share_src),
        (tgt_parts, layout[1], tgt_all, tgt_pos[0], share_tgt),
    ):
        for part, offsets in zip(parts, offsets_list):
            for k, offset in enumerate(offsets):
                start = pl.multiple_of((pos ^ offset) * share, share)
                copies.append(
                    pltpu.make_async_copy(
                        part.at[pl.ds(k * share, share)], dest.at[pl.ds(start, share)], sem.at[len(copies)]
                    )
                )
    for copy in copies:
        copy.start()
    top[...] = jnp.full(top.shape, sentinel, jnp.float32)
    tot[...] = jnp.zeros(tot.shape, jnp.float32)
    for copy in copies:
        copy.wait()

    def product(s):
        r = pl.multiple_of(rows_at[s] * BLOCK, BLOCK)
        c = pl.multiple_of(cols_at[s] * BLOCK, BLOCK)
        dot = lax.dot_general(
            tgt_all[pl.ds(c, BLOCK), :],
            src_all[pl.ds(r, BLOCK), :],
            (((1,), (1,)), ((), ())),
            preferred_element_type=jnp.float32,
        )
        scores[s] = dot * (inv_temp * log2e)

    def reduce(s):
        row_step(scores[s], rows_at[s], top, tot)

    n = count[0]
    product(0)

    def body(s, carry):
        product(s)
        reduce(s - 1)
        return carry

    lax.fori_loop(1, n, body, 0)
    reduce(n - 1)
    finish_rows(top, tot, lse)


def row_step(shifted, r, top, tot):
    tall = shifted.reshape(BLOCK // SUB, SUB, BLOCK)
    at = pl.ds(pl.multiple_of(r * SUB, SUB), SUB)
    old = top[at, :]
    new = jnp.maximum(old, jnp.max(tall, axis=0))
    sums = jnp.sum(jnp.exp2(tall - new[None]), axis=0)
    tot[at, :] = tot[at, :] * jnp.exp2(old - new) + sums
    top[at, :] = new


def finish_rows(top, tot, lse):
    tops = top[...].reshape(ROW_BLOCKS, SUB, BLOCK)
    best = jnp.max(tops, axis=1, keepdims=True)
    total = jnp.sum(tot[...].reshape(ROW_BLOCKS, SUB, BLOCK) * jnp.exp2(tops - best), axis=1)
    best = best.reshape(ROW_BLOCKS, BLOCK)
    lse[...] = jnp.where(best > 0.5 * sentinel, best + jnp.log2(total), sentinel)


def spread_cols(duals, wide):
    for n in range(COL_BLOCKS):
        wide[pl.ds(n * BLOCK, BLOCK), :] = jnp.broadcast_to(duals[n : n + 1, :], (LANES, BLOCK)).T


def row_kernel(meta, scores, cols, lse, wide, top, tot):
    rows_at, cols_at, count = meta
    top[...] = jnp.full(top.shape, sentinel, jnp.float32)
    tot[...] = jnp.zeros(tot.shape, jnp.float32)
    spread_cols(cols[...], wide)

    def body(s, carry):
        col = wide[pl.ds(pl.multiple_of(cols_at[s] * BLOCK, BLOCK), BLOCK), :]
        shifted = scores[s] + jnp.concatenate([col, col], axis=1)
        row_step(shifted, rows_at[s], top, tot)
        return carry

    lax.fori_loop(0, count[0], body, 0)
    finish_rows(top, tot, lse)


def col_kernel(meta, scores, rows, lse, top, tot):
    rows_at, cols_at, count = meta
    top[...] = jnp.full(top.shape, sentinel, jnp.float32)
    tot[...] = jnp.zeros(tot.shape, jnp.float32)

    def body(s, carry):
        at = pl.ds(pl.multiple_of(cols_at[s] * BLOCK, BLOCK), BLOCK)
        shifted = scores[s] + rows[pl.ds(rows_at[s], 1), :]
        low, high = shifted[:, :LANES], shifted[:, LANES:]
        old = top[at, :]
        new = jnp.maximum(old, jnp.maximum(low, high))
        tot[at, :] = tot[at, :] * jnp.exp2(old - new) + (jnp.exp2(low - new) + jnp.exp2(high - new))
        top[at, :] = new
        return carry

    lax.fori_loop(0, count[0], body, 0)
    tops = top[...].reshape(COL_BLOCKS, BLOCK, LANES)
    for n in range(COL_BLOCKS):
        flat = tops[n].T
        best = jnp.max(flat, axis=0, keepdims=True)
        total = jnp.sum(tot[pl.ds(n * BLOCK, BLOCK), :].T * jnp.exp2(flat - best), axis=0, keepdims=True)
        lse[pl.ds(n, 1), :] = best + jnp.log2(total)


def plan_kernel(meta, scores, rows, cols, out, wide, hold, sem):
    rows_at, cols_at, count = meta
    slots = out.shape[0]
    spread_cols(cols[...], wide)
    n = count[0]

    def put(s):
        return pltpu.make_async_copy(hold.at[s], out.at[s], sem)

    def body(s, carry):
        col = wide[pl.ds(pl.multiple_of(cols_at[s] * BLOCK, BLOCK), BLOCK), :]
        shifted = scores[s] + jnp.concatenate([col, col], axis=1) + rows[pl.ds(rows_at[s], 1), :]
        hold[s] = jnp.exp2(shifted).T.astype(jnp.bfloat16)
        put(s).start()
        return carry

    lax.fori_loop(0, n, body, 0)

    def blank(s, carry):
        hold[s] = jnp.zeros((BLOCK, BLOCK), jnp.bfloat16)
        put(s).start()
        return carry

    lax.fori_loop(n, slots, blank, 0)
    pltpu.make_async_copy(hold, out, sem).wait()


def split_meta(kernel, n_meta):
    def wrapped(*refs):
        return kernel(refs[:n_meta], *refs[n_meta:])

    return wrapped


def shards(src_emb, tgt_emb, block_rows, block_cols, block_counts):
    rows_at, cols_at = block_rows[0, 0], block_cols[0, 0]
    count = block_counts[0]
    slots = rows_at.shape[0]
    share_src, share_tgt = src_emb.shape[0], tgt_emb.shape[0]
    n_src, n_tgt = lax.axis_size("src"), lax.axis_size("tgt")
    src_unit, tgt_unit = unit_rows(src_emb), unit_rows(tgt_emb)
    src_held = gather_rows(src_unit, "tgt")
    tgt_held = gather_rows(tgt_unit, "src")
    layout = ([o for o, _ in src_held], [o for o, _ in tgt_held])
    pos = (lax.axis_index("tgt").reshape(1), lax.axis_index("src").reshape(1))
    meta = (rows_at, cols_at, count)
    f32 = jnp.float32
    wide = pltpu.VMEM((COL_BLOCKS * BLOCK, LANES), f32)
    row_acc = pltpu.VMEM((ROW_BLOCKS * SUB, BLOCK), f32)
    row_shape = jax.ShapeDtypeStruct((ROW_BLOCKS, BLOCK), f32)
    col_shape = jax.ShapeDtypeStruct((COL_BLOCKS, BLOCK), f32)
    n_copies = sum(len(o) for o in layout[0]) + sum(len(o) for o in layout[1])

    scores, lse = pl.pallas_call(
        split_meta(functools.partial(first_pass_kernel, layout, share_src, share_tgt), 5),
        in_specs=[SM] * 5 + [ANY] * (len(src_held) + len(tgt_held)),
        out_specs=[VM, VM],
        out_shape=[jax.ShapeDtypeStruct((slots, BLOCK, BLOCK), f32), row_shape],
        scratch_shapes=[
            pltpu.VMEM((ROW_BLOCKS * BLOCK, BLOCK), jnp.bfloat16),
            pltpu.VMEM((COL_BLOCKS * BLOCK, BLOCK), jnp.bfloat16),
            row_acc,
            row_acc,
            pltpu.SemaphoreType.DMA((n_copies,)),
        ],
        compiler_params=pltpu.CompilerParams(vmem_limit_bytes=24 << 20),
        name="first_rows",
    )(*meta, *pos, *[r for _, r in src_held], *[r for _, r in tgt_held])

    row_call = pl.pallas_call(
        split_meta(row_kernel, 3),
        in_specs=[SM] * 3 + [VM, VM],
        out_specs=VM,
        out_shape=row_shape,
        scratch_shapes=[wide, row_acc, row_acc],
        compiler_params=pltpu.CompilerParams(vmem_limit_bytes=24 << 20),
        name="rows",
    )
    col_call = pl.pallas_call(
        split_meta(col_kernel, 3),
        in_specs=[SM] * 3 + [VM, VM],
        out_specs=VM,
        out_shape=col_shape,
        scratch_shapes=[wide, wide],
        compiler_params=pltpu.CompilerParams(vmem_limit_bytes=24 << 20),
        name="cols",
    )
    log_ratio = math.log2(ROW_BLOCKS * n_src / (COL_BLOCKS * n_tgt))
    for sweep in range(ITERS):
        if sweep:
            lse = row_call(*meta, scores, col_dual)
        row_dual = -total_lse(lse, "tgt")
        col_dual = log_ratio - total_lse(col_call(*meta, scores, row_dual), "src")
    transport = pl.pallas_call(
        split_meta(plan_kernel, 3),
        in_specs=[SM] * 3 + [VM, VM, VM],
        out_specs=ANY,
        out_shape=jax.ShapeDtypeStruct((slots, BLOCK, BLOCK), jnp.bfloat16),
        scratch_shapes=[wide, pltpu.VMEM((slots, BLOCK, BLOCK), jnp.bfloat16), pltpu.SemaphoreType.DMA],
        compiler_params=pltpu.CompilerParams(vmem_limit_bytes=24 << 20),
        name="plan",
    )(*meta, scores, row_dual, col_dual)

    def own(dual, axis):
        width = dual.size // lax.axis_size(axis)
        part = lax.dynamic_slice_in_dim(dual.reshape(-1), lax.axis_index(axis) * width, width)
        return part * (ln2 / inv_temp)

    return (transport[None, None], own(row_dual, "tgt"), own(col_dual, "src"))


def solution(mesh):
    return jax.shard_map(
        shards,
        mesh=mesh,
        in_specs=(
            P(("src", "tgt"), None),
            P(("tgt", "src"), None),
            P("src", "tgt", None),
            P("src", "tgt", None),
            P("src", "tgt"),
        ),
        out_specs=(P("src", "tgt", None, None, None), P(("src", "tgt")), P(("tgt", "src"))),
        check_vma=False,
    )
```
